256 devices in a mesh: replica: 64 (over y, z, core), fsdp: 4 (over x).
Axes of the slice: x: 4, y: 4, z: 8, core: 2. Of those that a mesh axis runs over, the one named last changes fastest.
Arguments:
- activations: bfloat16 [64, 4096, 4096], P('replica', 'fsdp')
- cotangents: bfloat16 [64, 4096, 512], P('replica', 'fsdp'), may hold values from -0.059814453 to 0.059814453
- momentum: float32 [64, 4096, 512], P('replica', 'fsdp'), may hold values from -6 to 6
- keep_index: int32 [64, 512, 32], P(None, 'fsdp'), may hold values from 0 to 4095, as said below
Outputs:
- new_momentum: float32 [64, 4096, 512], P('replica', 'fsdp')
- update: bfloat16 [4096, 512], P('fsdp')
The draws below stay inside these ranges and needn't reach their ends.
Inputs may be any that keep to these rules, and one draw needn't show every extreme that they name: keep_index[r, t, j] lies in [j * 64 * 2, (j + 1) * 64 * 2), so a tile's indices are distinct and ascending.
All inputs are finite; a program needn't handle non-finite values.
Results may differ from the reference program's by a relative error of at most 0.013.
Values may be sent and summed in bfloat16 or wider, within the bound.
A program may use at most 128 MiB of HBM per device.

```python
import math
import jax
import jax.numpy as jnp
from jax import lax

D_WIN = 4096
KV_WIN = 512
TILE = 64
KEEP = 32
REPLICAS = 64
TOK_REP = 4096
TILES = 512


def draw_activations(key, part):
    key_scale = jax.random.fold_in(key, 11)
    key_value = jax.random.fold_in(key, 12)
    column_scale = jnp.exp(jax.random.uniform(key_scale, (D_WIN,), jnp.float32, 0.0, math.log(10.0)))
    values = jax.random.normal(key_value, (REPLICAS, TOK_REP, D_WIN), jnp.float32)
    return (values * column_scale).astype(jnp.bfloat16)


def draw_keep_index(key, part):
    band = TILE * TILE // KEEP
    offsets = jax.random.randint(jax.random.fold_in(key, 21), (REPLICAS, TILES, KEEP), 0, band, jnp.int32)
    return offsets + jnp.arange(KEEP).astype(jnp.int32) * band


def levels(stream_key, dims, split, smallest, top_value):
    loudness = 1.0
    for dim, parts in split:
        draws = jax.random.uniform(jax.random.fold_in(jax.random.fold_in(stream_key, 6), dim), (parts,), jnp.float32, smallest / len(split), top_value / len(split))
        loudness = loudness * jnp.repeat(jnp.exp(draws), dims[dim] // parts).reshape((-1,) + (1,) * (len(dims) - 1 - dim))
    return loudness


def normal_values(key, extent, deviation, limit, split=(), dtype=jnp.bfloat16):
    gain = levels(key, extent, split, -0.22, 0.18) if split else 1.0
    result = jax.random.normal(key, extent, jnp.float32) * deviation * gain
    return jnp.minimum(jnp.maximum(result, -limit), limit).astype(dtype)


def setup_inputs(seed: int = 0) -> dict:
    key_list = jax.random.split(jax.random.key(seed), 5)
    activations = draw_activations(jax.random.fold_in(key_list[4], 71), 0)
    cotangents = normal_values(key_list[1], (REPLICAS, TOK_REP, KV_WIN), 0.01, 0.059814453, ((0, 64), (1, 4)))
    momentum = normal_values(key_list[2], (REPLICAS, D_WIN, KV_WIN), 1.0, 6.0, ((0, 64), (1, 4)), jnp.float32)
    keep_index = draw_keep_index(jax.random.fold_in(key_list[4], 71), 0)
    return {"activations": activations, "cotangents": cotangents, "momentum": momentum, "keep_index": keep_index}


BETA = 0.999
EPS = 1e-06
highest = lax.Precision.HIGHEST

def cosine_table():
    sample = jnp.arange(TILE).astype(jnp.float32)
    freq_index = sample[:, None]
    table = jnp.cos(jnp.pi * (2.0 * sample[None, :] + 1.0) * freq_index / (2.0 * TILE))
    weight_row = jnp.where(freq_index == 0, jnp.sqrt(1.0 / TILE), jnp.sqrt(2.0 / TILE))
    return (table * weight_row).astype(jnp.float32)

def forward_tiles(matrix, cosine):
    row_count, col_count = matrix.shape
    blocks = matrix.reshape(row_count // TILE, TILE, col_count // TILE, TILE)
    left = jnp.einsum('ka,iajb->ikjb', cosine, blocks, precision=highest)
    return jnp.einsum('ikjb,lb->ikjl', left, cosine, precision=highest).reshape(row_count, col_count)

def inverse_tiles(matrix, cosine):
    row_count, col_count = matrix.shape
    blocks = matrix.reshape(row_count // TILE, TILE, col_count // TILE, TILE)
    left = jnp.einsum('ka,ikjl->iajl', cosine, blocks, precision=highest)
    return jnp.einsum('iajl,lb->iajb', left, cosine, precision=highest).reshape(row_count, col_count)

def flat_positions(indices, col_count):
    tile_count = indices.shape[-2]
    tile_cols = col_count // TILE
    tile_id = jnp.arange(tile_count).astype(jnp.int32)[:, None]
    tile_row = tile_id // tile_cols
    tile_col = tile_id % tile_cols
    freq_row = indices // TILE
    freq_col = indices % TILE
    return ((tile_row * TILE + freq_row) * tile_cols + tile_col) * TILE + freq_col

def reference(activations, cotangents, momentum, keep_index):
    cosine = cosine_table()

    def one_replica(running, inputs):
        tokens_here, grads_here, moment_old, indices = inputs
        gradient = lax.dot_general(tokens_here, grads_here, (((0,), (0,)), ((), ())), preferred_element_type=jnp.float32)
        moment = BETA * moment_old + gradient
        spectrum = forward_tiles(moment, cosine).reshape(-1)
        where_flat = flat_positions(indices, KV_WIN).reshape(-1)
        sent_grid = jnp.zeros_like(spectrum).at[where_flat].add(spectrum[where_flat])
        new_moment = moment - inverse_tiles(sent_grid.reshape(moment.shape), cosine)
        return (running + sent_grid, new_moment)
    start_sum = jnp.zeros((D_WIN * KV_WIN,), jnp.float32)
    summed, new_momentum = lax.scan(one_replica, start_sum, (activations, cotangents, momentum, keep_index))
    merged = inverse_tiles(summed.reshape(D_WIN, KV_WIN), cosine) / REPLICAS
    square_total = jnp.sum(merged * merged)
    scale_factor = lax.rsqrt(square_total / (D_WIN * KV_WIN) + EPS)
    return (new_momentum, (merged * scale_factor).astype(jnp.bfloat16))
```

```python
import functools

import jax
import jax.numpy as jnp
import numpy as np
from jax import lax
from jax.experimental import pallas as pl
from jax.experimental.pallas import tpu as pltpu
from jax.sharding import Mesh
from jax.sharding import PartitionSpec as P

D_WIN = 4096
KV_WIN = 512
TILE = 64
KEEP = 32
REPLICA = ("y", "z", "c")
BETA = 0.999
EPS = 1e-06
NX, NY, NZ, NC = 4, 4, 8, 2
NR = NY * NZ * NC
TOK = 1024
ROWS = D_WIN // NX
HALF = ROWS // 2
CH = 128
C = HALF // CH
SKEW = 2
MESH = pl.DeviceIdType.MESH
F32, BF16 = jnp.float32, jnp.bfloat16
NN = (((1,), (0,)), ((), ()))
NT = (((1,), (1,)), ((), ()))
TN = (((0,), (0,)), ((), ()))


def tables():
    n = np.arange(TILE, dtype=np.float64)
    cosine = np.cos(np.pi * (2.0 * n[None, :] + 1.0) * n[:, None] / (2.0 * TILE))
    cosine *= np.where(n[:, None] == 0, np.sqrt(1.0 / TILE), np.sqrt(2.0 / TILE))
    cosine = cosine.astype(np.float32)
    forward = np.kron(np.eye(4, dtype=np.float32), cosine)
    merge = [
        np.kron(np.eye(4, dtype=np.float32), cosine[b::2]) / np.float32(NR)
        for b in range(2)
    ]
    parts = [forward, forward.T, np.concatenate(merge)]
    out = []
    for part in parts:
        head = part.astype(jnp.bfloat16)
        out += [head, (part - head.astype(np.float32)).astype(jnp.bfloat16)]
    return np.concatenate(out)


def mm(a, b, dims=NN):
    return lax.dot_general(a, b, dims, preferred_element_type=F32)


def split(x):
    head = x.astype(BF16)
    return head, (x - head.astype(F32)).astype(BF16)


def left3(head, rest, x):
    xh, xl = split(x)
    return mm(head, xh) + mm(head, xl) + mm(rest, xh)


def right3(x, head, rest):
    xh, xl = split(x)
    return mm(xh, head) + mm(xl, head) + mm(xh, rest)


def iota(shape, dim):
    return lax.broadcasted_iota(jnp.int32, shape, dim)


def kernel(
    act, cot, mom, keep, cst, out_m, out_u,
    actv, cotv, momv, keepv, kown, cstv, bmat, psum_v, offs,
    send, recv, newm, vz, vy, upd, ufin, sqacc, sqbuf,
    act_sem, in_sem, mom_sem, rs_send, rs_recv, z_send, z_recv, y_send, y_recv,
    sw_send, sw_recv, n_send, n_recv, om_sem, ou_sem,
):
    y, z, c, x = (lax.axis_index(a) for a in ("y", "z", "c", "x"))
    me = (y * NZ + z) * NC + c

    def block_of(h, d):
        return lax.rem(jnp.where(d == 0, x + 3 * (1 + h), x + 1 + h), NX)

    def act_copy(h, d, k):
        col = block_of(h, d) * ROWS + d * HALF + k * CH
        return pltpu.make_async_copy(
            act.at[0, :, pl.ds(pl.multiple_of(col, CH), CH)],
            actv.at[h, d, k],
            act_sem.at[h, d, k],
        )

    def mom_copy(d, k):
        row = pl.multiple_of(d * HALF + k * CH, CH)
        return pltpu.make_async_copy(
            mom.at[0, pl.ds(row, CH)], momv.at[d, k], mom_sem.at[d, k]
        )

    small = [
        pltpu.make_async_copy(cot.at[0], cotv, in_sem.at[0]),
        pltpu.make_async_copy(cst, cstv, in_sem.at[1]),
        pltpu.make_async_copy(keep.at[me], kown, in_sem.at[2]),
        pltpu.make_async_copy(
            keep.at[:, pl.ds(pl.multiple_of(c * 64, 64), 64)], keepv, in_sem.at[3]
        ),
    ]
    small[0].start()

    def start_act(i, _):
        h, k, d = i // (2 * C), lax.rem(i // 2, C), lax.rem(i, 2)
        act_copy(h, d, k).start()
        return _

    lax.fori_loop(0, 2 * C, start_act, 0)

    barrier = pltpu.get_barrier_semaphore()
    peers = []
    for i in range(1, NX * NC):
        o = lax.rem(x * NC + c + i, NX * NC)
        peers.append({"x": o // NC, "c": lax.rem(o, NC)})
    z_peers = [{"z": lax.rem(z + i, NZ)} for i in range(1, NZ)]
    y_peers = []
    for i in range(1, NY * NC):
        o = lax.rem(y * NC + c + i, NY * NC)
        y_peers.append((o // NC, lax.rem(o, NC)))
    for dev in peers + z_peers + [{"y": a, "c": b} for a, b in y_peers]:
        pl.semaphore_signal(barrier, inc=1, device_id=dev, device_id_type=MESH)

    for copy in small[1:3]:
        copy.start()
    lax.fori_loop(2 * C, 8 * C, start_act, 0)

    def start_mom(i, _):
        mom_copy(lax.rem(i, 2), i // 2).start()
        return _

    lax.fori_loop(0, 2 * C, start_mom, 0)
    small[3].start()

    bmat[...] = (iota((16, 512), 0) % 8 == iota((16, 512), 1) // TILE).astype(F32).astype(BF16)
    ki, li = iota((128, 256), 0), iota((128, 256), 1)
    psum_v[...] = (
        ((ki // 64) == (li // 128)) & ((ki % 64) // 2 == li % 32)
    ).astype(F32).astype(BF16)
    sqacc[...] = jnp.zeros_like(sqacc)

    def rs_copy(h, d, k):
        to = lax.rem(jnp.where(d == 0, x + 1, x + 3), NX)
        return pltpu.make_async_remote_copy(
            src_ref=send.at[h, d, k],
            dst_ref=recv.at[h, d, k],
            send_sem=rs_send.at[h, d, k],
            recv_sem=rs_recv.at[h, d, k],
            device_id={"x": to},
            device_id_type=MESH,
        )

    def own_part(h, d, k):
        act_copy(h, d, k).wait()
        return mm(actv[h, d, k], cotv[...], TN)

    def first(k):
        def one(d, _):
            send[0, d, k] = own_part(0, d, k).astype(BF16)
            rs_copy(0, d, k).start()
            return _

        lax.fori_loop(0, 2, one, 0)

    def hop(h, k):
        def one(d, _):
            part = own_part(h, d, k)
            rs_copy(h - 1, d, k).wait_recv()
            send[h, d, k] = (part + recv[h - 1, d, k].astype(F32)).astype(BF16)
            rs_copy(h, d, k).start()
            return _

        lax.fori_loop(0, 2, one, 0)

    def z_copy(k, i):
        return pltpu.make_async_remote_copy(
            src_ref=vz.at[k, :, z],
            dst_ref=vz.at[k, :, z],
            send_sem=z_send.at[k, i - 1],
            recv_sem=z_recv.at[k, i - 1],
            device_id={"z": lax.rem(z + i, NZ)},
            device_id_type=MESH,
        )

    def y_copy(k, i):
        a, b = y_peers[i - 1]
        return pltpu.make_async_remote_copy(
            src_ref=vz.at[k, b],
            dst_ref=vy.at[k, y * NC + c],
            send_sem=y_send.at[k, i - 1],
            recv_sem=y_recv.at[k, i - 1],
            device_id={"y": a, "c": b},
            device_id_type=MESH,
        )

    def swap_copy(k):
        row = pl.ds(pl.multiple_of(c * HALF + k * CH, CH), CH)
        return pltpu.make_async_remote_copy(
            src_ref=upd.at[row],
            dst_ref=upd.at[row],
            send_sem=sw_send.at[k],
            recv_sem=sw_recv.at[k],
            device_id={"c": 1 - c},
            device_id_type=MESH,
        )

    def norm_copy(i):
        return pltpu.make_async_remote_copy(
            src_ref=sqbuf.at[x * NC + c],
            dst_ref=sqbuf.at[x * NC + c],
            send_sem=n_send.at[i - 1],
            recv_sem=n_recv.at[i - 1],
            device_id=peers[i - 1],
            device_id_type=MESH,
        )

    def out_copy(d, k):
        row = pl.multiple_of(d * HALF + k * CH, CH)
        return pltpu.make_async_copy(
            newm.at[d, k], out_m.at[0, pl.ds(row, CH)], om_sem.at[d, k]
        )

    fh, fl = cstv.at[0:256], cstv.at[256:512]
    th, tl = cstv.at[512:768], cstv.at[768:1024]
    qh, ql = cstv.at[1024:1280], cstv.at[1280:1536]

    def finish(k):
        def one(d, _):
            part = own_part(3, d, k)
            mom_copy(d, k).wait()
            rs_copy(2, d, k).wait_recv()
            moment = BETA * momv[d, k] + (part + recv[2, d, k].astype(F32))
            half = left3(fh[0:128, 0:128], fl[0:128, 0:128], moment)
            spec = jnp.concatenate(
                [right3(half[:, i : i + 256], th[...], tl[...]) for i in (0, 256)], axis=1
            )
            base = pl.multiple_of(d * 64 + k * 16, 16)
            own = (kown[pl.ds(base, 16), :] - iota((16, KEEP), 1) * 128).astype(F32)
            pick = (iota((128, KEEP), 0) % 64 // 2 == iota((128, KEEP), 1)).astype(F32)
            rows = mm(pick.astype(BF16), own.astype(BF16), NT)
            same = iota((128, 16), 0) // 64 == iota((128, 16), 1) // 8
            slot = mm(jnp.where(same, rows, 0.0).astype(BF16), bmat[...])
            here = (iota((128, 512), 0) % 2 * 64 + iota((128, 512), 1) % 64).astype(F32)
            sent = jnp.where(slot == here, spec, 0.0)
            back = left3(th[0:128, 0:128], tl[0:128, 0:128], sent)
            newm[d, k] = moment - jnp.concatenate(
                [right3(back[:, i : i + 256], fh[...], fl[...]) for i in (0, 256)], axis=1
            )
            out_copy(d, k).start()
            sh, sl = split(sent)
            bm = bmat[0:8, :]
            by_row = mm(bm, sh, NT) + mm(bm, sl, NT)
            bh, bl = split(by_row)
            by_band = mm(bh, psum_v[...]) + mm(bl, psum_v[...])
            ti, lane = iota((8, 256), 0), iota((8, 256), 1)
            by_band = jnp.where(lane % 128 // 32 == ti // 2, by_band, 0.0)
            for q in range(2):
                line = jnp.sum(
                    jnp.where(ti % 2 == q, by_band, 0.0), axis=0, keepdims=True
                )
                for t in range(2):
                    vz[k, d, z, pl.ds(2 * t + q, 1), :] = line[:, t * 128 : t * 128 + 128]
            return _

        lax.fori_loop(0, 2, one, 0)
        for i in range(1, NZ):
            z_copy(k, i).start()

    def spread(k):
        for i in range(1, NZ):
            z_copy(k, i).wait_recv()
        for i in range(1, NY * NC):
            y_copy(k, i).start()
        vy[k, y * NC + c] = vz[k, c]

    def gather_offsets():
        small[3].wait()
        band = iota((8, 128), 1) % 32 * 128

        def one(r, _):
            for q in range(2):
                parts = [keepv[r, pl.ds(2 * m + q, 8, stride=8), :] for m in range(4)]
                offs[r, pl.ds(8 * q, 8), :] = jnp.concatenate(parts, axis=1) - band
            return _

        lax.fori_loop(0, NR, one, 0)

    def merge(k):
        for i in range(1, NY * NC):
            y_copy(k, i).wait_recv()
        place = iota((128, 128), 0)
        for t in range(2):
            sides = []
            for q in range(2):
                line = 8 * q + 2 * k + t

                def add(g, total, line=line, t=t, q=q):
                    a, b = g // NC, lax.rem(g, NC)
                    for zz in range(NZ):
                        r = (a * NZ + zz) * NC + b
                        o = offs[r, pl.ds(line, 1), :]
                        v = vy[k, g, zz, pl.ds(2 * t + q, 1), :]
                        total += jnp.where(o == place, v, 0.0)
                    return total

                total = lax.fori_loop(0, NY * NC, add, jnp.zeros((128, 128), F32))
                left = left3(th[0:128, 0:128], tl[0:128, 0:128], total)
                sides.append(
                    right3(left[0:64], qh[0:128], ql[0:128])
                    + right3(left[64:128], qh[128:256], ql[128:256])
                )
            tiles = jnp.concatenate(sides, axis=0).T
            row = pl.ds(pl.multiple_of(c * HALF + k * CH + t * 64, 64), 64)
            for m in range(4):
                piece = tiles[m * 64 : m * 64 + 64]
                upd[row, m * 128 : m * 128 + 128] = piece.astype(BF16)
                sqacc[...] += jnp.sum((piece * piece).reshape(8, 8, 128), axis=0)
        swap_copy(k).start()

    def step(t, carry):
        for h, unit in ((0, first), (1, hop), (2, hop), (3, finish)):
            k = t - SKEW * h

            @pl.when((k >= 0) & (k < C))
            def _(h=h, k=k, unit=unit):
                unit(h, k) if unit is hop else unit(k)

        @pl.when(t == 2)
        def _():
            gather_offsets()

        k1 = t - SKEW * 3 - 1

        @pl.when((k1 >= 0) & (k1 < C))
        def _():
            spread(k1)

        k2 = t - SKEW * 3 - 2

        @pl.when((k2 >= 0) & (k2 < C))
        def _():
            merge(k2)

        return carry

    small[0].wait()
    small[1].wait()
    small[2].wait()
    n_peers = len(peers) + len(z_peers) + len(y_peers)
    pl.semaphore_wait(barrier, n_peers)
    lax.fori_loop(0, C + SKEW * 3 + 2, step, 0)

    sqbuf[x * NC + c] = sqacc[...]
    for i in range(1, NX * NC):
        norm_copy(i).start()
    for k in range(C):
        swap_copy(k).wait_recv()
    for i in range(1, NX * NC):
        norm_copy(i).wait_recv()
    total = jnp.sum(jnp.sum(sqbuf[...], axis=0), keepdims=True)
    scale = lax.rsqrt(total / (D_WIN * KV_WIN) + EPS)

    def u_copy(i):
        row = pl.ds(pl.multiple_of(i * 128, 128), 128)
        return pltpu.make_async_copy(ufin.at[row], out_u.at[row], ou_sem.at[i])

    def scaled(i, _):
        row = pl.ds(pl.multiple_of(i * 128, 128), 128)
        ufin[row] = (upd[row].astype(F32) * scale).astype(BF16)
        u_copy(i).start()
        return _

    lax.fori_loop(0, ROWS // 128, scaled, 0)

    def drain(k, _):
        for d in range(2):
            out_copy(d, k).wait()
            for h in range(3):
                rs_copy(h, d, k).wait_send()
        for i in range(1, NZ):
            z_copy(k, i).wait_send()
        for i in range(1, NY * NC):
            y_copy(k, i).wait_send()
        swap_copy(k).wait_send()
        return _

    lax.fori_loop(0, C, drain, 0)
    for i in range(1, NX * NC):
        norm_copy(i).wait_send()
    lax.fori_loop(0, ROWS // 128, lambda i, _: (u_copy(i).wait(), _)[1], 0)


def shards(activations, cotangents, momentum, keep_index):
    constants = jnp.asarray(tables())
    dma = pltpu.SemaphoreType.DMA
    vmem = pltpu.VMEM
    return pl.pallas_call(
        kernel,
        out_shape=(
            jax.ShapeDtypeStruct((1, ROWS, KV_WIN), F32),
            jax.ShapeDtypeStruct((ROWS, KV_WIN), BF16),
        ),
        in_specs=[pl.BlockSpec(memory_space=pl.ANY)] * 5,
        out_specs=[pl.BlockSpec(memory_space=pl.ANY)] * 2,
        scratch_shapes=[
            vmem((4, 2, C, TOK, CH), BF16),
            vmem((TOK, KV_WIN), BF16),
            vmem((2, C, CH, KV_WIN), F32),
            vmem((NR, 64, KEEP), jnp.int32),
            vmem((128, KEEP), jnp.int32),
            vmem((1536, 256), BF16),
            vmem((16, 512), BF16),
            vmem((128, 256), BF16),
            vmem((NR, 16, 128), jnp.int32),
            vmem((3, 2, C, CH, KV_WIN), BF16),
            vmem((3, 2, C, CH, KV_WIN), BF16),
            vmem((2, C, CH, KV_WIN), F32),
            vmem((C, 2, NZ, 4, 128), F32),
            vmem((C, NY * NC, NZ, 4, 128), F32),
            vmem((ROWS, KV_WIN), BF16),
            vmem((ROWS, KV_WIN), BF16),
            vmem((8, 128), F32),
            vmem((NX * NC, 8, 128), F32),
            dma((4, 2, C)),
            dma((4,)),
            dma((2, C)),
            dma((3, 2, C)),
            dma((3, 2, C)),
            dma((C, NZ - 1)),
            dma((C, NZ - 1)),
            dma((C, NY * NC - 1)),
            dma((C, NY * NC - 1)),
            dma((C,)),
            dma((C,)),
            dma((NX * NC - 1,)),
            dma((NX * NC - 1,)),
            dma((2, C)),
            dma((ROWS // 128,)),
        ],
        compiler_params=pltpu.CompilerParams(
            collective_id=0, has_side_effects=True, vmem_limit_bytes=56 * 2**20
        ),
    )(activations, cotangents, momentum, keep_index, constants)


def solution(mesh):
    split_mesh = Mesh(
        mesh.devices.reshape(NY, NZ, NC, NX),
        ("y", "z", "c", "x"),
    )
    in_specs = (
        P(REPLICA, "x", None),
        P(REPLICA, "x", None),
        P(REPLICA, "x", None),
        P(None, "x", None),
    )
    out_specs = (P(REPLICA, "x", None), P("x", None))
    return jax.shard_map(
        shards, mesh=split_mesh, in_specs=in_specs, out_specs=out_specs, check_vma=False
    )
```

```python
import functools

import jax
import jax.numpy as jnp
import numpy as np
from jax import lax
from jax.experimental import pallas as pl
from jax.experimental.pallas import tpu as pltpu
from jax.sharding import Mesh
from jax.sharding import PartitionSpec as P

D_WIN = 4096
KV_WIN = 512
TILE = 64
KEEP = 32
REPLICA = ("y", "z", "c")
BETA = 0.999
EPS = 1e-06
NX, NY, NZ, NC = 4, 4, 8, 2
NR = NY * NZ * NC
TOK = 1024
ROWS = D_WIN // NX
HALF = ROWS // 2
CH = 128
C = HALF // CH
FIRST = (0, 1, 4, 5)
HOP1 = (2, 3, 7, 8)
HOP2 = (4, 5, 9, 10)
FINISH = (6, 7, 10, 11)
SPREAD = (7, 9, 11, 12)
MERGE = (9, 11, 12, 13)
MESH = pl.DeviceIdType.MESH
F32, BF16 = jnp.float32, jnp.bfloat16
NN = (((1,), (0,)), ((), ()))
NT = (((1,), (1,)), ((), ()))
TN = (((0,), (0,)), ((), ()))


def tables():
    n = np.arange(TILE, dtype=np.float64)
    cosine = np.cos(np.pi * (2.0 * n[None, :] + 1.0) * n[:, None] / (2.0 * TILE))
    cosine *= np.where(n[:, None] == 0, np.sqrt(1.0 / TILE), np.sqrt(2.0 / TILE))
    cosine = cosine.astype(np.float32)
    forward = np.kron(np.eye(4, dtype=np.float32), cosine)
    merge = [
        np.kron(np.eye(4, dtype=np.float32), cosine[b::2]) / np.float32(NR)
        for b in range(2)
    ]
    parts = [forward, forward.T, np.concatenate(merge)]
    out = []
    for part in parts:
        head = part.astype(jnp.bfloat16)
        out += [head, (part - head.astype(np.float32)).astype(jnp.bfloat16)]
    return np.concatenate(out)


def mm(a, b, dims=NN):
    return lax.dot_general(a, b, dims, preferred_element_type=F32)


def split(x):
    head = x.astype(BF16)
    return head, (x - head.astype(F32)).astype(BF16)


def left3(both, x):
    xh, xl = split(x)
    n = both.shape[0] // 2
    wide = mm(both, xh)
    return wide[:n] + wide[n:] + mm(both[:n], xl)


def right3(x, head, rest):
    xh, xl = split(x)
    n = x.shape[0]
    tall = mm(jnp.concatenate([xh, xl], axis=0), head)
    return tall[:n] + tall[n:] + mm(xh, rest)


def iota(shape, dim):
    return lax.broadcasted_iota(jnp.int32, shape, dim)


def kernel(
    act, cot, mom, keep, cst, out_m, upd, out_s,
    actv, cotv, momv, keepv, cstv, pick_v, bmat, over_v, psum_v, offs,
    send, recv, vz, vy, sqacc, sqbuf,
    act_sem, in_sem, mom_sem, rs_send, rs_recv, z_send, z_recv, y_send, y_recv,
    sw_send, sw_recv, n_send, n_recv,
):
    y, z, c, x = (lax.axis_index(a) for a in ("y", "z", "c", "x"))
    me = (y * NZ + z) * NC + c

    def block_of(h, d):
        return lax.rem(jnp.where(d == 0, x + 3 * (1 + h), x + 1 + h), NX)

    def act_copy(h, d, k):
        col = block_of(h, d) * ROWS + d * HALF + k * CH
        return pltpu.make_async_copy(
            act.at[0, :, pl.ds(pl.multiple_of(col, CH), CH)],
            actv.at[h, k, :, pl.ds(pl.multiple_of(d * CH, CH), CH)],
            act_sem.at[h, d, k],
        )

    def mom_copy(d, k):
        row = pl.multiple_of(d * HALF + k * CH, CH)
        return pltpu.make_async_copy(
            mom.at[0, pl.ds(row, CH)], momv.at[d, k], mom_sem.at[d, k]
        )

    small = [
        pltpu.make_async_copy(cst, cstv, in_sem.at[0]),
        pltpu.make_async_copy(keep, keepv, in_sem.at[1]),
        pltpu.make_async_copy(cot.at[0], cotv, in_sem.at[2]),
    ]

    barrier = pltpu.get_barrier_semaphore()
    peers = []
    for i in range(1, NX * NC):
        o = lax.rem(x * NC + c + i, NX * NC)
        peers.append({"x": o // NC, "c": lax.rem(o, NC)})
    z_peers = [{"z": lax.rem(z + i, NZ)} for i in range(1, NZ)]
    y_peers = []
    for i in range(1, NY * NC):
        o = lax.rem(y * NC + c + i, NY * NC)
        y_peers.append((o // NC, lax.rem(o, NC)))
    for dev in peers + z_peers + [{"y": a, "c": b} for a, b in y_peers]:
        pl.semaphore_signal(barrier, inc=1, device_id=dev, device_id_type=MESH)

    def start_act(i, carry):
        h, k, d = i // (2 * C), lax.rem(i // 2, C), lax.rem(i, 2)
        act_copy(h, d, k).start()
        return carry

    small[2].start()
    lax.fori_loop(0, 2 * C, start_act, 0)
    small[0].start()
    small[1].start()
    lax.fori_loop(2 * C, 8 * C, start_act, 0)

    def start_mom(i, carry):
        mom_copy(lax.rem(i, 2), i // 2).start()
        return carry

    lax.fori_loop(0, 2 * C, start_mom, 0)

    def prepare():
        one = lambda mask: mask.astype(F32).astype(BF16)
        bmat[...] = one(iota((8, 256), 0) == iota((8, 256), 1) // TILE)
        over_v[...] = one(iota((128, 256), 0) % 4 == iota((128, 256), 1) // TILE)
        ki, li = iota((512, 512), 0), iota((512, 512), 1)
        psum_v[...] = one(
            (ki % 256 // 64 == li // 128)
            & (ki % 64 // 2 == li % 32)
            & (ki // 256 == li % 128 // 64)
        )
        row, tile = iota((64, 128), 0), iota((64, 128), 1)
        part, row = row // 16, row % 16
        want = c * 64 + row // 4 * 16 + row // 2 % 2 * 8 + part * 2 + row % 2
        pick_v[...] = one(want == tile)
        sqacc[...] = jnp.zeros_like(sqacc)

    def rs_copy(h, d, k):
        to = lax.rem(jnp.where(d == 0, x + 1, x + 3), NX)
        return pltpu.make_async_remote_copy(
            src_ref=send.at[h, d, k],
            dst_ref=recv.at[h, d, k],
            send_sem=rs_send.at[h, d, k],
            recv_sem=rs_recv.at[h, d, k],
            device_id={"x": to},
            device_id_type=MESH,
        )

    def own_part(h, k):
        for d in range(2):
            act_copy(h, d, k).wait()
        return mm(actv[h, k], cotv[...], TN)

    def first(k):
        part = own_part(0, k).astype(BF16)
        for d in range(2):
            send[0, d, k] = part[d * CH : d * CH + CH]
            rs_copy(0, d, k).start()

    def hop(h, k):
        part = own_part(h, k)
        for d in range(2):
            rs_copy(h - 1, d, k).wait_recv()
            mine = part[d * CH : d * CH + CH]
            send[h, d, k] = (mine + recv[h - 1, d, k].astype(F32)).astype(BF16)
            rs_copy(h, d, k).start()

    def z_copy(k, i):
        return pltpu.make_async_remote_copy(
            src_ref=vz.at[k, :, z],
            dst_ref=vz.at[k, :, z],
            send_sem=z_send.at[k, i - 1],
            recv_sem=z_recv.at[k, i - 1],
            device_id={"z": lax.rem(z + i, NZ)},
            device_id_type=MESH,
        )

    def y_copy(k, i):
        a, b = y_peers[i - 1]
        return pltpu.make_async_remote_copy(
            src_ref=vz.at[k, b],
            dst_ref=vy.at[k, y * NC + c],
            send_sem=y_send.at[k, i - 1],
            recv_sem=y_recv.at[k, i - 1],
            device_id={"y": a, "c": b},
            device_id_type=MESH,
        )

    def swap_copy(k):
        row = pl.ds(pl.multiple_of(c * HALF + k * CH, CH), CH)
        return pltpu.make_async_remote_copy(
            src_ref=upd.at[row],
            dst_ref=upd.at[row],
            send_sem=sw_send.at[k],
            recv_sem=sw_recv.at[k],
            device_id={"c": 1 - c},
            device_id_type=MESH,
        )

    def norm_copy(i):
        return pltpu.make_async_remote_copy(
            src_ref=sqbuf.at[x * NC + c],
            dst_ref=sqbuf.at[x * NC + c],
            send_sem=n_send.at[i - 1],
            recv_sem=n_recv.at[i - 1],
            device_id=peers[i - 1],
            device_id_type=MESH,
        )

    fh, fl = cstv.at[0:256], cstv.at[256:512]
    th, tl = cstv.at[512:768], cstv.at[768:1024]
    qh, ql = cstv.at[1024:1280], cstv.at[1280:1536]

    def finish(k):
        @pl.when(k == 0)
        def _():
            small[0].wait()
            small[1].wait()

        part = own_part(3, k)
        for d in range(2):
            mom_copy(d, k).wait()
        own = (keepv[me] - iota((KEEP, 128), 0) * 128).astype(F32).astype(BF16)
        pick = (iota((64, KEEP), 0) // 2 == iota((64, KEEP), 1)).astype(F32).astype(BF16)
        slot = jnp.concatenate([mm(pick, own)] * 8, axis=0)
        ki, tile = iota((512, 128), 0), iota((512, 128), 1)
        slab, d, tr = ki // 256, ki // 128 % 2, ki // 64 % 2
        mine = (tile // 8 == d * 8 + k * 2 + tr) & (tile % 8 // 4 == slab)
        slot = mm(jnp.where(mine, slot, 0.0).astype(BF16), over_v[...])
        here = (iota((512, 256), 0) % 2 * 64 + iota((512, 256), 1) % TILE).astype(F32)
        old = jnp.concatenate([momv[0, k], momv[1, k]], axis=0)
        for d in range(2):
            rs_copy(2, d, k).wait_recv()
        got = jnp.concatenate([recv[2, 0, k], recv[2, 1, k]], axis=0).astype(F32)
        moment = BETA * old + (part + got)
        half = left3(cstv[0:512], moment)
        half = jnp.concatenate([half[:, 0:256], half[:, 256:512]], axis=0)
        sent = jnp.where(slot == here, right3(half, th[...], tl[...]), 0.0)
        by_row = mm(bmat[...], sent.astype(BF16), NT).astype(BF16)
        by_band = mm(by_row, psum_v[...])
        ti, lane = iota((8, 512), 0), iota((8, 512), 1)
        by_band = jnp.where(lane % 64 // 32 == ti // 2, by_band, 0.0)
        for q in range(2):
            line = jnp.sum(jnp.where(ti % 2 == q, by_band, 0.0), axis=0, keepdims=True)
            for d in range(2):
                for t in range(2):
                    at = d * 256 + t * 128
                    vz[k, d, z, 2 * t + q : 2 * t + q + 1, :] = line[:, at : at + 128]
        for i in range(1, NZ):
            z_copy(k, i).start()
        back = right3(sent, fh[...], fl[...])
        back = jnp.concatenate([back[0:256], back[256:512]], axis=1)
        new = moment - left3(cstv[512:1024], back)
        for d in range(2):
            row = pl.ds(pl.multiple_of(d * HALF + k * CH, CH), CH)
            out_m[0, row] = new[d * CH : d * CH + CH]

    def spread(k):
        for i in range(1, NZ):
            z_copy(k, i).wait_recv()
        for i in range(1, NY * NC):
            y_copy(k, i).start()
        vy[k, y * NC + c] = vz[k, c]

    def gather_offsets():
        def one(i, carry):
            four = keepv[pl.ds(4 * i, 4)] - iota((4, KEEP, 128), 1) * 128
            four = four.reshape(4 * KEEP, 128).astype(F32).astype(BF16)
            got = mm(pick_v[...], four, NT)
            for r in range(4):
                parts = [
                    got[16 * p : 16 * p + 16, 32 * r : 32 * r + 32] for p in range(4)
                ]
                offs[4 * i + r] = jnp.concatenate(parts, axis=1)
            return carry

        lax.fori_loop(0, NR // 4, one, 0, unroll=8)

    def merge(k):
        for i in range(1, NY * NC):
            y_copy(k, i).wait_recv()
        place = iota((128, 128), 0).astype(F32).astype(BF16)
        none = jnp.zeros((128, 128), BF16)
        totals = []
        for t in range(2):

            def add(g, pair, t=t):
                a, b = g // NC, lax.rem(g, NC)
                pair = list(pair)
                for zz in range(0, NZ, 4):
                    for q in range(2):
                        hits = []
                        for z4 in range(zz, zz + 4):
                            r = (a * NZ + z4) * NC + b
                            o = offs[r, pl.ds(4 * k + 2 * t + q, 1), :]
                            v = vy[k, g, z4, 2 * t + q : 2 * t + q + 1, :]
                            o, v = (
                                jnp.broadcast_to(w, (16, 128)).astype(BF16) for w in (o, v)
                            )
                            o, v = (jnp.concatenate([w] * 8, axis=0) for w in (o, v))
                            hits.append(jnp.where(o == place, v, none))
                        four = (hits[0] + hits[1]) + (hits[2] + hits[3])
                        pair[q] += four.astype(F32)
                return tuple(pair)

            zero = jnp.zeros((128, 128), F32)
            totals += lax.fori_loop(0, NY * NC, add, (zero, zero))
        square = sum(jnp.sum((a * a).reshape(16, 8, 128), axis=0) for a in totals)
        sqacc[...] += square

        @pl.when(k == C - 1)
        def _():
            sqbuf[x * NC + c] = sqacc[...]
            for i in range(1, NX * NC):
                norm_copy(i).start()

        table = jnp.concatenate([th[0:128, 0:128], tl[0:128, 0:128]], axis=0)
        left = left3(table, jnp.concatenate(totals, axis=1))
        left = jnp.concatenate(
            [
                jnp.concatenate([left[0:64, i : i + 128], left[64:128, i : i + 128]], axis=1)
                for i in range(0, 512, 128)
            ],
            axis=0,
        )
        both = right3(left, qh[...], ql[...])
        for t in range(2):
            tiles = both[t * 128 : t * 128 + 128].T
            row = pl.ds(pl.multiple_of(c * HALF + k * CH + t * 64, 64), 64)
            for m in range(4):
                piece = tiles[m * 64 : m * 64 + 64]
                upd[row, m * 128 : m * 128 + 128] = piece.astype(BF16)
        swap_copy(k).start()

    def step(t, carry):
        def at(times, unit):
            hit = [t == when for when in times]
            k = sum(jnp.where(h, i, 0) for i, h in enumerate(hit))

            @pl.when(functools.reduce(jnp.logical_or, hit))
            def _():
                unit(k)

        at(HOP2, functools.partial(hop, 2))
        at(HOP1, functools.partial(hop, 1))
        at(FIRST, first)
        at(FINISH, finish)

        @pl.when(t == 1)
        def _():
            prepare()

        @pl.when(t == 6)
        def _():
            gather_offsets()

        at(SPREAD, spread)
        at(MERGE, merge)
        return carry

    small[2].wait()
    pl.semaphore_wait(barrier, len(peers) + len(z_peers) + len(y_peers))
    lax.fori_loop(0, MERGE[-1] + 1, step, 0)

    def drain(k, carry):
        for d in range(2):
            for h in range(3):
                rs_copy(h, d, k).wait_send()
        for i in range(1, NZ):
            z_copy(k, i).wait_send()
        for i in range(1, NY * NC):
            y_copy(k, i).wait_send()
        swap_copy(k).wait_send()
        return carry

    lax.fori_loop(0, C, drain, 0)
    for k in range(C):
        swap_copy(k).wait_recv()
    for i in range(1, NX * NC):
        norm_copy(i).wait_recv()
    for i in range(1, NX * NC):
        norm_copy(i).wait_send()
    total = jnp.sum(jnp.sum(sqbuf[...], axis=0), keepdims=True)
    out_s[...] = jnp.broadcast_to(
        lax.rsqrt(total / (NR * NR) / (D_WIN * KV_WIN) + EPS), (8, 128)
    )


def write_out(new_v, upd_v, scale_v, out_m, out_u, done, m_sem, u_sem):
    half = ROWS // 2
    m_copies = [
        pltpu.make_async_copy(
            new_v.at[0, i * half : i * half + half],
            out_m.at[0, i * half : i * half + half],
            m_sem.at[i],
        )
        for i in range(2)
    ]
    for copy in m_copies:
        copy.start()
    scale = scale_v[0:1, 0:1]
    part = ROWS // 4
    u_copies = []
    for i in range(4):
        row = slice(i * part, i * part + part)
        done[row] = (upd_v[row].astype(F32) * scale).astype(BF16)
        u_copies.append(pltpu.make_async_copy(done.at[row], out_u.at[row], u_sem.at[i]))
        u_copies[-1].start()
    for copy in m_copies + u_copies:
        copy.wait()


def shards(activations, cotangents, momentum, keep_index):
    operands = (
        activations,
        cotangents,
        momentum,
        keep_index.swapaxes(1, 2),
        jnp.asarray(tables()),
    )
    dma = pltpu.SemaphoreType.DMA
    vmem = pltpu.VMEM
    new, update, scale = pl.pallas_call(
        kernel,
        out_shape=(
            jax.ShapeDtypeStruct((1, ROWS, KV_WIN), F32),
            jax.ShapeDtypeStruct((ROWS, KV_WIN), BF16),
            jax.ShapeDtypeStruct((8, 128), F32),
        ),
        in_specs=[pl.BlockSpec(memory_space=pl.ANY)] * 5,
        out_specs=[pl.BlockSpec(memory_space=pltpu.VMEM)] * 3,
        scratch_shapes=[
            vmem((4, C, TOK, 2 * CH), BF16),
            vmem((TOK, KV_WIN), BF16),
            vmem((2, C, CH, KV_WIN), F32),
            vmem((NR, KEEP, 128), jnp.int32),
            vmem((1536, 256), BF16),
            vmem((64, 128), BF16),
            vmem((8, 256), BF16),
            vmem((128, 256), BF16),
            vmem((512, 512), BF16),
            vmem((NR, 16, 128), F32),
            vmem((3, 2, C, CH, KV_WIN), BF16),
            vmem((3, 2, C, CH, KV_WIN), BF16),
            vmem((C, 2, NZ, 4, 128), F32),
            vmem((C, NY * NC, NZ, 4, 128), F32),
            vmem((8, 128), F32),
            vmem((NX * NC, 8, 128), F32),
            dma((4, 2, C)),
            dma((3,)),
            dma((2, C)),
            dma((3, 2, C)),
            dma((3, 2, C)),
            dma((C, NZ - 1)),
            dma((C, NZ - 1)),
            dma((C, NY * NC - 1)),
            dma((C, NY * NC - 1)),
            dma((C,)),
            dma((C,)),
            dma((NX * NC - 1,)),
            dma((NX * NC - 1,)),
        ],
        compiler_params=pltpu.CompilerParams(
            collective_id=0, has_side_effects=True, vmem_limit_bytes=48 * 2**20
        ),
    )(*(pltpu.with_memory_space_constraint(a, pltpu.HBM) for a in operands))
    return pl.pallas_call(
        write_out,
        out_shape=(
            jax.ShapeDtypeStruct((1, ROWS, KV_WIN), F32),
            jax.ShapeDtypeStruct((ROWS, KV_WIN), BF16),
        ),
        in_specs=[pl.BlockSpec(memory_space=pltpu.VMEM)] * 3,
        out_specs=[pl.BlockSpec(memory_space=pl.ANY)] * 2,
        scratch_shapes=[vmem((ROWS, KV_WIN), BF16), dma((2,)), dma((4,))],
        compiler_params=pltpu.CompilerParams(vmem_limit_bytes=16 * 2**20),
    )(new, update, scale)


def solution(mesh):
    split_mesh = Mesh(
        mesh.devices.reshape(NY, NZ, NC, NX),
        ("y", "z", "c", "x"),
    )
    in_specs = (
        P(REPLICA, "x", None),
        P(REPLICA, "x", None),
        P(REPLICA, "x", None),
        P(None, "x", None),
    )
    out_specs = (P(REPLICA, "x", None), P("x", None))
    return jax.shard_map(
        shards, mesh=split_mesh, in_specs=in_specs, out_specs=out_specs, check_vma=False
    )
```

```python
import functools

import jax
import jax.numpy as jnp
import numpy as np
from jax import lax
from jax.experimental import pallas as pl
from jax.experimental.pallas import tpu as pltpu
from jax.sharding import Mesh
from jax.sharding import PartitionSpec as P

D_WIN = 4096
KV_WIN = 512
TILE = 64
KEEP = 32
REPLICA = ("y", "z", "c")
BETA = 0.999
EPS = 1e-06
NX, NY, NZ, NC = 4, 4, 8, 2
NR = NY * NZ * NC
TOK = 1024
ROWS = D_WIN // NX
HALF = ROWS // 2
CH = 128
C = HALF // CH
FIRST = (0, 1, 4, 5)
HOP1 = (2, 3, 7, 8)
HOP2 = (4, 5, 9, 10)
FINISH = (6, 7, 10, 11)
SPREAD = (7, 9, 11, 12)
MERGE = (9, 11, 12, 13)
MESH = pl.DeviceIdType.MESH
F32, BF16 = jnp.float32, jnp.bfloat16
NN = (((1,), (0,)), ((), ()))
NT = (((1,), (1,)), ((), ()))
TN = (((0,), (0,)), ((), ()))


def tables():
    n = np.arange(TILE, dtype=np.float64)
    cosine = np.cos(np.pi * (2.0 * n[None, :] + 1.0) * n[:, None] / (2.0 * TILE))
    cosine *= np.where(n[:, None] == 0, np.sqrt(1.0 / TILE), np.sqrt(2.0 / TILE))
    cosine = cosine.astype(np.float32)
    forward = np.kron(np.eye(4, dtype=np.float32), cosine)
    merge = [
        np.kron(np.eye(4, dtype=np.float32), cosine[b::2]) / np.float32(NR)
        for b in range(2)
    ]
    parts = [forward, forward.T, np.concatenate(merge)]
    out = []
    for part in parts:
        head = part.astype(jnp.bfloat16)
        out += [head, (part - head.astype(np.float32)).astype(jnp.bfloat16)]
    return np.concatenate(out)


def mm(a, b, dims=NN):
    return lax.dot_general(a, b, dims, preferred_element_type=F32)


def split(x):
    head = x.astype(BF16)
    return head, (x - head.astype(F32)).astype(BF16)


def left3(both, x):
    xh, xl = split(x)
    n = both.shape[0] // 2
    wide = mm(both, xh)
    return wide[:n] + wide[n:] + mm(both[:n], xl)


def right3(x, head, rest):
    xh, xl = split(x)
    n = x.shape[0]
    tall = mm(jnp.concatenate([xh, xl], axis=0), head)
    return tall[:n] + tall[n:] + mm(xh, rest)


def iota(shape, dim):
    return lax.broadcasted_iota(jnp.int32, shape, dim)


def kernel(
    act, cot, mom, keep, cst, out_m, upd, out_s,
    actv, cotv, momv, keepv, cstv, pick_v, bmat, over_v, psum_v, offs,
    send, recv, vz, vy, sqacc, sqbuf,
    act_sem, in_sem, mom_sem, rs_send, rs_recv, z_send, z_recv, y_send, y_recv,
    sw_send, sw_recv, n_send, n_recv,
):
    y, z, c, x = (lax.axis_index(a) for a in ("y", "z", "c", "x"))
    me = (y * NZ + z) * NC + c

    def block_of(h, d):
        return lax.rem(jnp.where(d == 0, x + 3 * (1 + h), x + 1 + h), NX)

    def act_copy(h, d, k):
        col = block_of(h, d) * ROWS + d * HALF + k * CH
        return pltpu.make_async_copy(
            act.at[0, :, pl.ds(pl.multiple_of(col, CH), CH)],
            actv.at[h, k, :, pl.ds(pl.multiple_of(d * CH, CH), CH)],
            act_sem.at[h, d, k],
        )

    def mom_copy(d, k):
        row = pl.multiple_of(d * HALF + k * CH, CH)
        return pltpu.make_async_copy(
            mom.at[0, pl.ds(row, CH)], momv.at[d, k], mom_sem.at[d, k]
        )

    small = [
        pltpu.make_async_copy(cst, cstv, in_sem.at[0]),
        pltpu.make_async_copy(keep, keepv, in_sem.at[1]),
        pltpu.make_async_copy(cot.at[0], cotv, in_sem.at[2]),
    ]

    barrier = pltpu.get_barrier_semaphore()
    peers = []
    for i in range(1, NX * NC):
        o = lax.rem(x * NC + c + i, NX * NC)
        peers.append({"x": o // NC, "c": lax.rem(o, NC)})
    z_peers = [{"z": lax.rem(z + i, NZ)} for i in range(1, NZ)]
    y_peers = []
    for i in range(1, NY * NC):
        o = lax.rem(y * NC + c + i, NY * NC)
        y_peers.append((o // NC, lax.rem(o, NC)))
    for dev in peers + z_peers + [{"y": a, "c": b} for a, b in y_peers]:
        pl.semaphore_signal(barrier, inc=1, device_id=dev, device_id_type=MESH)

    def start_act(i, carry):
        h, k, d = i // (2 * C), lax.rem(i // 2, C), lax.rem(i, 2)
        act_copy(h, d, k).start()
        return carry

    small[2].start()
    lax.fori_loop(0, 2 * C, start_act, 0)
    small[0].start()
    small[1].start()
    lax.fori_loop(2 * C, 8 * C, start_act, 0)

    def start_mom(i, carry):
        mom_copy(lax.rem(i, 2), i // 2).start()
        return carry

    lax.fori_loop(0, 2 * C, start_mom, 0)

    def prepare():
        one = lambda mask: mask.astype(F32).astype(BF16)
        bmat[...] = one(iota((8, 256), 0) == iota((8, 256), 1) // TILE)
        over_v[...] = one(iota((128, 256), 0) % 4 == iota((128, 256), 1) // TILE)
        ki, li = iota((512, 512), 0), iota((512, 512), 1)
        psum_v[...] = one(
            (ki % 256 // 64 == li // 128)
            & (ki % 64 // 2 == li % 32)
            & (ki // 256 == li % 128 // 64)
        )
        row, tile = iota((64, 128), 0), iota((64, 128), 1)
        part, row = row // 16, row % 16
        want = c * 64 + row // 4 * 16 + row // 2 % 2 * 8 + part * 2 + row % 2
        pick_v[...] = one(want == tile)
        sqacc[...] = jnp.zeros_like(sqacc)

    def rs_copy(h, d, k):
        to = lax.rem(jnp.where(d == 0, x + 1, x + 3), NX)
        return pltpu.make_async_remote_copy(
            src_ref=send.at[h, d, k],
            dst_ref=recv.at[h, d, k],
            send_sem=rs_send.at[h, d, k],
            recv_sem=rs_recv.at[h, d, k],
            device_id={"x": to},
            device_id_type=MESH,
        )

    def own_part(h, k):
        for d in range(2):
            act_copy(h, d, k).wait()
        return mm(actv[h, k], cotv[...], TN)

    def first_part(k):
        part = own_part(0, k).astype(BF16)
        for d in range(2):
            send[0, d, k] = part[d * CH : d * CH + CH]

    def first_send(k):
        for d in range(2):
            rs_copy(0, d, k).start()

    def first(k):
        first_part(k)
        first_send(k)

    def hop(h, k):
        part = own_part(h, k)
        for d in range(2):
            rs_copy(h - 1, d, k).wait_recv()
            mine = part[d * CH : d * CH + CH]
            send[h, d, k] = (mine + recv[h - 1, d, k].astype(F32)).astype(BF16)
            rs_copy(h, d, k).start()

    def z_copy(k, i):
        return pltpu.make_async_remote_copy(
            src_ref=vz.at[k, :, z],
            dst_ref=vz.at[k, :, z],
            send_sem=z_send.at[k, i - 1],
            recv_sem=z_recv.at[k, i - 1],
            device_id={"z": lax.rem(z + i, NZ)},
            device_id_type=MESH,
        )

    def y_copy(k, i):
        a, b = y_peers[i - 1]
        return pltpu.make_async_remote_copy(
            src_ref=vz.at[k, b],
            dst_ref=vy.at[k, y * NC + c],
            send_sem=y_send.at[k, i - 1],
            recv_sem=y_recv.at[k, i - 1],
            device_id={"y": a, "c": b},
            device_id_type=MESH,
        )

    def swap_copy(k):
        row = pl.ds(pl.multiple_of(c * HALF + k * CH, CH), CH)
        return pltpu.make_async_remote_copy(
            src_ref=upd.at[row],
            dst_ref=upd.at[row],
            send_sem=sw_send.at[k],
            recv_sem=sw_recv.at[k],
            device_id={"c": 1 - c},
            device_id_type=MESH,
        )

    def norm_copy(i):
        return pltpu.make_async_remote_copy(
            src_ref=sqbuf.at[x * NC + c],
            dst_ref=sqbuf.at[x * NC + c],
            send_sem=n_send.at[i - 1],
            recv_sem=n_recv.at[i - 1],
            device_id=peers[i - 1],
            device_id_type=MESH,
        )

    fh, fl = cstv.at[0:256], cstv.at[256:512]
    th, tl = cstv.at[512:768], cstv.at[768:1024]
    qh, ql = cstv.at[1024:1280], cstv.at[1280:1536]

    def finish(k):
        @pl.when(k == 0)
        def _():
            small[0].wait()
            small[1].wait()

        part = own_part(3, k)
        for d in range(2):
            mom_copy(d, k).wait()
        own = (keepv[me] - iota((KEEP, 128), 0) * 128).astype(F32).astype(BF16)
        pick = (iota((64, KEEP), 0) // 2 == iota((64, KEEP), 1)).astype(F32).astype(BF16)
        slot = jnp.concatenate([mm(pick, own)] * 8, axis=0)
        ki, tile = iota((512, 128), 0), iota((512, 128), 1)
        slab, d, tr = ki // 256, ki // 128 % 2, ki // 64 % 2
        mine = (tile // 8 == d * 8 + k * 2 + tr) & (tile % 8 // 4 == slab)
        slot = mm(jnp.where(mine, slot, 0.0).astype(BF16), over_v[...])
        here = (iota((512, 256), 0) % 2 * 64 + iota((512, 256), 1) % TILE).astype(F32)
        old = jnp.concatenate([momv[0, k], momv[1, k]], axis=0)
        for d in range(2):
            rs_copy(2, d, k).wait_recv()
        got = jnp.concatenate([recv[2, 0, k], recv[2, 1, k]], axis=0).astype(F32)
        moment = BETA * old + (part + got)
        half = left3(cstv[0:512], moment)
        half = jnp.concatenate([half[:, 0:256], half[:, 256:512]], axis=0)
        sent = jnp.where(slot == here, right3(half, th[...], tl[...]), 0.0)
        by_row = mm(bmat[...], sent.astype(BF16), NT).astype(BF16)
        by_band = mm(by_row, psum_v[...])
        ti, lane = iota((8, 512), 0), iota((8, 512), 1)
        by_band = jnp.where(lane % 64 // 32 == ti // 2, by_band, 0.0)
        for q in range(2):
            line = jnp.sum(jnp.where(ti % 2 == q, by_band, 0.0), axis=0, keepdims=True)
            for d in range(2):
                for t in range(2):
                    at = d * 256 + t * 128
                    vz[k, d, z, 2 * t + q : 2 * t + q + 1, :] = line[:, at : at + 128]
        for i in range(1, NZ):
            z_copy(k, i).start()
        back = right3(sent, fh[...], fl[...])
        back = jnp.concatenate([back[0:256], back[256:512]], axis=1)
        new = moment - left3(cstv[512:1024], back)
        for d in range(2):
            row = pl.ds(pl.multiple_of(d * HALF + k * CH, CH), CH)
            out_m[0, row] = new[d * CH : d * CH + CH]

    def spread(k):
        for i in range(1, NZ):
            z_copy(k, i).wait_recv()
        for i in range(1, NY * NC):
            y_copy(k, i).start()
        vy[k, y * NC + c] = vz[k, c]

    def gather_offsets():
        def one(i, carry):
            four = keepv[pl.ds(4 * i, 4)] - iota((4, KEEP, 128), 1) * 128
            four = four.reshape(4 * KEEP, 128).astype(F32).astype(BF16)
            got = mm(pick_v[...], four, NT)
            for r in range(4):
                parts = [
                    got[16 * p : 16 * p + 16, 32 * r : 32 * r + 32] for p in range(4)
                ]
                offs[4 * i + r] = jnp.concatenate(parts, axis=1)
            return carry

        lax.fori_loop(0, NR // 4, one, 0, unroll=8)

    def merge(k):
        for i in range(1, NY * NC):
            y_copy(k, i).wait_recv()
        place = iota((128, 128), 0).astype(F32).astype(BF16)
        none = jnp.zeros((128, 128), BF16)
        totals = []
        for t in range(2):

            def add(g, pair, t=t):
                a, b = g // NC, lax.rem(g, NC)
                pair = list(pair)
                for zz in range(0, NZ, 4):
                    for q in range(2):
                        hits = []
                        for z4 in range(zz, zz + 4):
                            r = (a * NZ + z4) * NC + b
                            o = offs[r, pl.ds(4 * k + 2 * t + q, 1), :]
                            v = vy[k, g, z4, 2 * t + q : 2 * t + q + 1, :]
                            o, v = (
                                jnp.broadcast_to(w, (16, 128)).astype(BF16) for w in (o, v)
                            )
                            o, v = (jnp.concatenate([w] * 8, axis=0) for w in (o, v))
                            hits.append(jnp.where(o == place, v, none))
                        four = (hits[0] + hits[1]) + (hits[2] + hits[3])
                        pair[q] += four.astype(F32)
                return tuple(pair)

            zero = jnp.zeros((128, 128), F32)
            totals += lax.fori_loop(0, NY * NC, add, (zero, zero))
        square = sum(jnp.sum((a * a).reshape(16, 8, 128), axis=0) for a in totals)
        sqacc[...] += square

        @pl.when(k == C - 1)
        def _():
            sqbuf[x * NC + c] = sqacc[...]
            for i in range(1, NX * NC):
                norm_copy(i).start()

        table = jnp.concatenate([th[0:128, 0:128], tl[0:128, 0:128]], axis=0)
        left = left3(table, jnp.concatenate(totals, axis=1))
        left = jnp.concatenate(
            [
                jnp.concatenate([left[0:64, i : i + 128], left[64:128, i : i + 128]], axis=1)
                for i in range(0, 512, 128)
            ],
            axis=0,
        )
        both = right3(left, qh[...], ql[...])
        for t in range(2):
            tiles = both[t * 128 : t * 128 + 128].T
            row = pl.ds(pl.multiple_of(c * HALF + k * CH + t * 64, 64), 64)
            for m in range(4):
                piece = tiles[m * 64 : m * 64 + 64]
                upd[row, m * 128 : m * 128 + 128] = piece.astype(BF16)
        swap_copy(k).start()

    def step(t, carry):
        def at(times, unit):
            hit = [t == when for when in times]
            k = sum(jnp.where(h, i, 0) for i, h in enumerate(hit))

            @pl.when(functools.reduce(jnp.logical_or, hit))
            def _():
                unit(k)

        at(HOP2, functools.partial(hop, 2))
        at(HOP1, functools.partial(hop, 1))
        at(FIRST, first)
        at(FINISH, finish)

        @pl.when(t == 6)
        def _():
            gather_offsets()

        at(SPREAD, spread)
        at(MERGE, merge)
        return carry

    small[2].wait()
    first_part(0)
    first_part(1)
    pl.semaphore_wait(barrier, len(peers) + len(z_peers) + len(y_peers))
    first_send(0)
    first_send(1)
    prepare()
    lax.fori_loop(2, MERGE[-1] + 1, step, 0)

    def drain(k, carry):
        for d in range(2):
            for h in range(3):
                rs_copy(h, d, k).wait_send()
        for i in range(1, NZ):
            z_copy(k, i).wait_send()
        for i in range(1, NY * NC):
            y_copy(k, i).wait_send()
        swap_copy(k).wait_send()
        return carry

    lax.fori_loop(0, C, drain, 0)
    for k in range(C):
        swap_copy(k).wait_recv()
    for i in range(1, NX * NC):
        norm_copy(i).wait_recv()
    for i in range(1, NX * NC):
        norm_copy(i).wait_send()
    total = jnp.sum(jnp.sum(sqbuf[...], axis=0), keepdims=True)
    out_s[...] = jnp.broadcast_to(
        lax.rsqrt(total / (NR * NR) / (D_WIN * KV_WIN) + EPS), (8, 128)
    )


def write_out(new_v, upd_v, scale_v, out_m, out_u, done, m_sem, u_sem):
    half = ROWS // 2
    m_copies = [
        pltpu.make_async_copy(
            new_v.at[0, i * half : i * half + half],
            out_m.at[0, i * half : i * half + half],
            m_sem.at[i],
        )
        for i in range(2)
    ]
    for copy in m_copies:
        copy.start()
    scale = scale_v[0:1, 0:1]
    part = ROWS // 4
    u_copies = []
    for i in range(4):
        row = slice(i * part, i * part + part)
        done[row] = (upd_v[row].astype(F32) * scale).astype(BF16)
        u_copies.append(pltpu.make_async_copy(done.at[row], out_u.at[row], u_sem.at[i]))
        u_copies[-1].start()
    for copy in m_copies + u_copies:
        copy.wait()


def shards(activations, cotangents, momentum, keep_index):
    operands = (
        activations,
        cotangents,
        momentum,
        keep_index.swapaxes(1, 2),
        jnp.asarray(tables()),
    )
    dma = pltpu.SemaphoreType.DMA
    vmem = pltpu.VMEM
    new, update, scale = pl.pallas_call(
        kernel,
        out_shape=(
            jax.ShapeDtypeStruct((1, ROWS, KV_WIN), F32),
            jax.ShapeDtypeStruct((ROWS, KV_WIN), BF16),
            jax.ShapeDtypeStruct((8, 128), F32),
        ),
        in_specs=[pl.BlockSpec(memory_space=pl.ANY)] * 5,
        out_specs=[pl.BlockSpec(memory_space=pltpu.VMEM)] * 3,
        scratch_shapes=[
            vmem((4, C, TOK, 2 * CH), BF16),
            vmem((TOK, KV_WIN), BF16),
            vmem((2, C, CH, KV_WIN), F32),
            vmem((NR, KEEP, 128), jnp.int32),
            vmem((1536, 256), BF16),
            vmem((64, 128), BF16),
            vmem((8, 256), BF16),
            vmem((128, 256), BF16),
            vmem((512, 512), BF16),
            vmem((NR, 16, 128), F32),
            vmem((3, 2, C, CH, KV_WIN), BF16),
            vmem((3, 2, C, CH, KV_WIN), BF16),
            vmem((C, 2, NZ, 4, 128), F32),
            vmem((C, NY * NC, NZ, 4, 128), F32),
            vmem((8, 128), F32),
            vmem((NX * NC, 8, 128), F32),
            dma((4, 2, C)),
            dma((3,)),
            dma((2, C)),
            dma((3, 2, C)),
            dma((3, 2, C)),
            dma((C, NZ - 1)),
            dma((C, NZ - 1)),
            dma((C, NY * NC - 1)),
            dma((C, NY * NC - 1)),
            dma((C,)),
            dma((C,)),
            dma((NX * NC - 1,)),
            dma((NX * NC - 1,)),
        ],
        compiler_params=pltpu.CompilerParams(
            collective_id=0, has_side_effects=True, vmem_limit_bytes=48 * 2**20
        ),
    )(*(pltpu.with_memory_space_constraint(a, pltpu.HBM) for a in operands))
    return pl.pallas_call(
        write_out,
        out_shape=(
            jax.ShapeDtypeStruct((1, ROWS, KV_WIN), F32),
            jax.ShapeDtypeStruct((ROWS, KV_WIN), BF16),
        ),
        in_specs=[pl.BlockSpec(memory_space=pltpu.VMEM)] * 3,
        out_specs=[pl.BlockSpec(memory_space=pl.ANY)] * 2,
        scratch_shapes=[vmem((ROWS, KV_WIN), BF16), dma((2,)), dma((4,))],
        compiler_params=pltpu.CompilerParams(vmem_limit_bytes=16 * 2**20),
    )(new, update, scale)


def solution(mesh):
    split_mesh = Mesh(
        mesh.devices.reshape(NY, NZ, NC, NX),
        ("y", "z", "c", "x"),
    )
    in_specs = (
        P(REPLICA, "x", None),
        P(REPLICA, "x", None),
        P(REPLICA, "x", None),
        P(None, "x", None),
    )
    out_specs = (P(REPLICA, "x", None), P("x", None))
    return jax.shard_map(
        shards, mesh=split_mesh, in_specs=in_specs, out_specs=out_specs, check_vma=False
    )
```
